32 devices in a mesh: visit: 8 (over z, y), patch: 4 (over x, core).
Axes of the slice: x: 2, y: 2, z: 4, core: 2. Of those that a mesh axis runs over, the one named last changes fastest.
Arguments:
- warped_tiles: bfloat16 [2048, 128, 128], P(('visit', 'patch')), may hold values from -12 to 12
- coefficients: bfloat16 [2048, 5], P(('visit', 'patch')), may hold values from -5 to 5
- tile_weight: bfloat16 [2048], P(('visit', 'patch')), may hold values from 0.01 to 0.15
- tile_cell: int32 [2048], P(('visit', 'patch')), may hold values from 0 to 63
- tile_valid: int32 [2048], P(('visit', 'patch')), may hold values 0 or 1
- dest_patch: int32 [2048], P(('visit', 'patch')), may hold values from 0 to 3, as said below
- basis_taps: bfloat16 [5, 2, 21], replicated, may hold values from -1.25 to 1.25
- filter_taps: bfloat16 [2, 41], replicated, may hold values from -1 to 1
Outputs:
- coadd_image: float32 [4, 1024, 1024], P('patch', 'visit')
- detection_map: float32 [4, 1024, 1024], P('patch', 'visit')
The draws below stay inside these ranges and needn't reach their ends.
Inputs may be any that keep to these rules, and one draw needn't show every extreme that they name: `dest_patch`: the 64 tiles of one device name at most 32 tiles for any one patch; in every draw one patch receives exactly 32 tiles from every device.
All inputs are finite; a program needn't handle non-finite values. No bound on the sum of `tile_valid` on one device may be relied on, other than what follows from the above.
Results may differ from the reference program's by a relative error of at most 0.0067.
Values may be sent and summed in bfloat16 or wider, within the bound.
No kernel may reach another device: no remote copies, remote signals or barrier semaphores. Data moves between devices by JAX's collectives and lax.ppermute only.
A program may use at most 64 MiB of HBM per device.

```python
import math
import jax
import jax.numpy as jnp
from jax import lax

TS = 128
TILES_DEV = 64
CELL_ROWS = 8
CELL_COLS = 8
NB = 5
HALF = 20
KT = 21
FT = 41
CAP = 32
TILES = 2048
CELLS = 64
PATCH_ROWS = 1024
PATCH_COLS = 1024
N_VISIT = 8
N_PATCH = 4


def draw_dest_patch(key, part):
    hot_patch = jax.random.randint(jax.random.fold_in(key, 7), (), 0, N_PATCH).astype(jnp.int32)
    pool_base = (jnp.arange((N_PATCH - 1) * CAP, dtype=jnp.int32) // CAP).astype(jnp.int32)
    pool = pool_base + (pool_base >= hot_patch).astype(jnp.int32)

    def one_block(block_key):
        first_key, second_key = jax.random.split(block_key)
        chosen = jax.random.permutation(first_key, pool)[:TILES_DEV - CAP]
        listing = jnp.concatenate([jnp.full((CAP,), hot_patch, jnp.int32), chosen])
        return jax.random.permutation(second_key, listing)
    block_keys = jax.random.split(jax.random.fold_in(key, 11), N_VISIT * N_PATCH)
    return jax.vmap(one_block)(block_keys).reshape(-1).astype(jnp.int32)


def draw_tile_weight(key, part):
    count = TILES_DEV * N_VISIT * N_PATCH
    position = jnp.arange(count, dtype=jnp.int32)
    group = (position // (TILES_DEV * N_PATCH)).astype(jnp.float32)
    rising = 1.0 + 2.0 * group / max(N_VISIT - 1, 1)
    base = jnp.exp(jax.random.uniform(key, (count,), jnp.float32, math.log(0.01), math.log(0.05)))
    return (base * rising).astype(jnp.bfloat16)


def with_ends(values, stream_key, smallest, high):
    spot = [jax.random.randint(jax.random.fold_in(stream_key, axis), (), 0, length) for axis, length in enumerate(values.shape)]
    main_axis = values.shape.index(max(values.shape))
    next_to = spot[:main_axis] + [(spot[main_axis] + 1) % values.shape[main_axis]] + spot[main_axis + 1:]
    return values.at[tuple(spot)].set(smallest).at[tuple(next_to)].set(high)


def levels(stream_key, extent, shards, least, largest):
    def one(axis_at, shards_of):
        heights = jax.random.uniform(jax.random.fold_in(jax.random.fold_in(stream_key, 6), axis_at), (shards_of,), jnp.float32, least / len(shards), largest / len(shards))
        return jnp.repeat(jnp.exp(heights), extent[axis_at] // shards_of).reshape((-1,) + (1,) * (len(extent) - axis_at - 1))

    level = one(*shards[0])
    for cut in shards[1:]:
        level = level * one(*cut)
    return level


def bell_draw(rng, shape, width, bound, cuts=(), kind=jnp.bfloat16):
    result = width * jax.random.normal(rng, shape, jnp.float32)
    if cuts:
        result = result * levels(rng, shape, cuts, -0.22, 0.18)
    return jnp.clip(result, -bound, bound).astype(kind)


def setup_inputs(seed: int = 0) -> dict:
    key_list = jax.random.split(jax.random.key(seed), 9)
    warped_tiles = bell_draw(key_list[0], (TILES, TS, TS), 2.0, 12.0, ((0, 32),))
    coefficients = bell_draw(key_list[1], (TILES, NB), 1.0, 5.0, ((0, 32),))
    tile_weight = draw_tile_weight(jax.random.fold_in(key_list[8], 71), 0)
    tile_cell = with_ends(jax.random.randint(key_list[3], (TILES,), 0, CELLS), jax.random.fold_in(key_list[3], 1), 0, CELLS - 1).astype(jnp.int32)
    tile_valid = with_ends((jax.random.randint(key_list[4], (TILES,), 0, 4) < 3).astype(jnp.int32), jax.random.fold_in(key_list[4], 1), 0, 1)
    dest_patch = draw_dest_patch(jax.random.fold_in(key_list[8], 71), 0)
    basis_taps = bell_draw(key_list[6], (NB, 2, KT), KT ** -0.5, 1.25)
    filter_taps = bell_draw(key_list[7], (2, FT), FT ** -0.5, 1.0)
    return {"warped_tiles": warped_tiles, "coefficients": coefficients, "tile_weight": tile_weight, "tile_cell": tile_cell, "tile_valid": tile_valid, "dest_patch": dest_patch, "basis_taps": basis_taps, "filter_taps": filter_taps}


def band_matrix(taps, nrows, ncols, shift):
    row_index = lax.broadcasted_iota(jnp.int32, (nrows, ncols), 0)
    col_index = lax.broadcasted_iota(jnp.int32, (nrows, ncols), 1)
    offset_map = col_index - row_index + shift
    total = jnp.zeros((nrows, ncols), taps.dtype)
    for position in range(taps.shape[0]):
        total = total + jnp.where(offset_map == position, taps[position], jnp.zeros((), taps.dtype))
    return total


def basis_mats(basis_taps, size):
    reach = (basis_taps.shape[2] - 1) // 2
    row_mats = []
    col_mats = []
    for basis in range(basis_taps.shape[0]):
        row_mats.append(band_matrix(basis_taps[basis, 0].astype(jnp.float32), size, size, reach))
        col_mats.append(band_matrix(basis_taps[basis, 1].astype(jnp.float32), size, size, reach).T)
    return jnp.stack(row_mats).astype(jnp.bfloat16), jnp.concatenate(col_mats, axis=1).astype(jnp.bfloat16)


def match_one(tile_data, scale_row, row_stack, col_joined):
    size = tile_data.shape[0]
    nbasis = row_stack.shape[0]
    columns_pass = jnp.dot(tile_data, col_joined, preferred_element_type=jnp.float32).reshape(size, nbasis, size)
    scaled = (columns_pass * scale_row.astype(jnp.float32)[None, :, None]).astype(jnp.bfloat16)
    summed = jnp.einsum('bik,kbj->ij', row_stack.astype(jnp.float32), scaled.astype(jnp.float32), precision=lax.Precision.HIGHEST)
    return summed.astype(jnp.bfloat16)


def reference(warped_tiles, coefficients, tile_weight, tile_cell, tile_valid, dest_patch, basis_taps, filter_taps):
    row_stack, col_joined = basis_mats(basis_taps, TS)
    effective = (tile_weight.astype(jnp.float32) * tile_valid.astype(jnp.float32)).astype(jnp.bfloat16)
    scales = (coefficients.astype(jnp.float32) * effective.astype(jnp.float32)[:, None]).astype(jnp.bfloat16)
    segment = (dest_patch * CELLS + tile_cell).astype(jnp.int32)
    blocks = TILES // 8

    def match_pair(tile_data, scale_row):
        return match_one(tile_data, scale_row, row_stack, col_joined)

    def accumulate(canvas, block):
        tiles_block, scales_block, segment_block = block
        matched = jax.vmap(match_pair)(tiles_block, scales_block)
        return canvas.at[segment_block].add(matched.astype(jnp.float32)), jnp.zeros((), jnp.float32)

    canvas_start = jnp.zeros((N_PATCH * CELLS, TS, TS), jnp.float32)
    canvas, unused = lax.scan(accumulate, canvas_start, (warped_tiles.reshape(blocks, 8, TS, TS), scales.reshape(blocks, 8, NB), segment.reshape(blocks, 8)))
    numerator = canvas.reshape(N_PATCH, CELL_ROWS, CELL_COLS, TS, TS).transpose(0, 1, 3, 2, 4).reshape(N_PATCH, PATCH_ROWS, PATCH_COLS)
    weight_sum = jax.ops.segment_sum(effective.astype(jnp.float32), segment, num_segments=N_PATCH * CELLS)
    weight_pixels = jnp.repeat(jnp.repeat(weight_sum.reshape(N_PATCH, CELL_ROWS, CELL_COLS), TS, axis=1), TS, axis=2)
    coadd_image = numerator / (weight_pixels + 1.0)
    coadd_rounded = coadd_image.astype(jnp.bfloat16)
    vertical_mat = band_matrix(filter_taps[0].astype(jnp.float32), PATCH_ROWS, PATCH_ROWS, HALF).astype(jnp.bfloat16)
    horizontal_mat = band_matrix(filter_taps[1].astype(jnp.float32), PATCH_COLS, PATCH_COLS, HALF).T.astype(jnp.bfloat16)

    def filter_one(plane):
        vertical = jnp.dot(vertical_mat, plane, preferred_element_type=jnp.float32).astype(jnp.bfloat16)
        return jnp.dot(vertical, horizontal_mat, preferred_element_type=jnp.float32)

    detection_map = lax.map(filter_one, coadd_rounded)
    return coadd_image, detection_map
```

```python
import functools

import jax
import jax.numpy as jnp
from jax import lax
from jax.experimental import pallas as pl
from jax.experimental.pallas import tpu as pltpu
from jax.sharding import PartitionSpec as P

CELL_ROWS = 8
CELL_COLS = 8
CELLS = CELL_ROWS * CELL_COLS
SETS = (((0, 2), (2, 4)), ((4, 6), (6, 8)))
UNROLL = 4
EDGE = 32
WROWS = 16
F32 = jnp.float32
BF16 = jnp.bfloat16


def in_vmem():
    return pl.BlockSpec(memory_space=pltpu.VMEM)


def in_smem():
    return pl.BlockSpec(memory_space=pltpu.SMEM)


def rows_shape(rows, dtype=BF16):
    return jax.ShapeDtypeStruct((rows, 128), dtype)


def band(get_tap, ntaps, nrows, ncols, shift, sign):
    row = lax.broadcasted_iota(jnp.int32, (nrows, ncols), 0)
    col = lax.broadcasted_iota(jnp.int32, (nrows, ncols), 1)
    offset = sign * (col - row) + shift
    out = jnp.zeros((nrows, ncols), F32)
    for k in range(ntaps):
        out = jnp.where(offset == k, get_tap(k), out)
    return out.astype(BF16)


def basis_kernel(taps, row_out, col_out, *, nb, nt, size):
    reach = (nt - 1) // 2
    for b in range(nb):
        row_out[b * size : (b + 1) * size, :] = band(
            lambda k: taps[(b * 2) * nt + k], nt, size, size, reach, 1
        )
        col_out[b * size : (b + 1) * size, :] = band(
            lambda k: taps[(b * 2 + 1) * nt + k], nt, size, size, reach, -1
        )


def filter_mats_kernel(taps, vert_out, horiz_out, *, nt, strip, pad):
    reach = (nt - 1) // 2
    vert_out[...] = band(lambda k: taps[k], nt, strip, strip + 2 * EDGE, reach - EDGE, 1)
    horiz_out[...] = band(lambda k: taps[nt + k], nt, pad * 2 + 128, 128, reach - pad, -1)


def split3(w):
    hi = w.astype(BF16)
    rest = w - hi.astype(F32)
    mid = rest.astype(BF16)
    lo = (rest - mid.astype(F32)).astype(BF16)
    return hi, mid, lo


def store_weights(ref, base, w):
    hi, mid, lo = (part.astype(F32) for part in split3(w))
    row = lax.broadcasted_iota(jnp.int32, (WROWS, 128), 0)
    block = jnp.where(row == 0, hi, jnp.where(row == 1, mid, jnp.where(row == 2, lo, 0.0)))
    ref[base : base + WROWS, :] = block.astype(BF16)


def load_weights(ref, base):
    block = ref[base : base + WROWS, :].astype(F32)
    return jnp.sum(block, axis=0, keepdims=True)


def match_kernel(
    scal,
    keys_own,
    keys_other,
    info_own,
    info_other,
    tiles_own,
    tiles_other,
    row_cat,
    col_cat,
    *refs,
    cfg,
    cols_a,
    cols_b,
):
    X, Y, Z, V, R, nb, count = cfg
    na, nbc = cols_a[1] - cols_a[0], cols_b[1] - cols_b[0]
    h0, h1 = cols_a[0], cols_b[1]
    a_out = refs[:X]
    b_out = refs[X : X + Y]
    acc, wacc, listing, tiles, sems = refs[X + Y :]
    size = tiles.shape[1]
    parts = size // R
    x, core, y = scal[0], scal[1], scal[3]
    copies = [
        pltpu.make_async_copy(tiles_own, tiles.at[pl.ds(0, count)], sems.at[0]),
        pltpu.make_async_copy(tiles_other, tiles.at[pl.ds(count, count)], sems.at[1]),
    ]
    for copy in copies:
        copy.start()
    acc[...] = jnp.zeros_like(acc)
    wacc[...] = jnp.zeros_like(wacc)

    def lister(keys, base):
        def body(t, n):
            key = keys[t]
            h = key & (CELL_COLS - 1)
            mine = (((key >> 6) & 1) == core) & (h >= h0) & (h < h1)
            listing[n] = base + t
            return n + mine.astype(jnp.int32)

        return body

    n = lax.fori_loop(0, count, lister(keys_own, 0), jnp.int32(0))
    n = lax.fori_loop(0, count, lister(keys_other, count), n)
    for q in range(UNROLL):
        listing[n + q] = 0
    for copy in copies:
        copy.wait()
    lane = lax.broadcasted_iota(jnp.int32, (1, 128), 1)

    def step(i, carry):
        todo = []
        for q in range(UNROLL):
            k = i * UNROLL + q
            live = k < n
            t = listing[k]
            own = t < count
            t_in = jnp.where(own, t, t - count)
            key = jnp.where(own, keys_own[t_in], keys_other[t_in])
            key = jnp.where(live, key, h0)
            values = [
                jnp.where(
                    live,
                    jnp.where(own, info_own[t_in * 8 + b], info_other[t_in * 8 + b]),
                    jnp.float32(0.0),
                )
                for b in range(nb + 1)
            ]
            todo.append((t, key, values))
        for q in range(0, UNROLL, 2):
            pair = todo[q : q + 2]
            wide = jnp.concatenate([tiles[t] for t, _, _ in pair], axis=1)
            rows = jnp.dot(row_cat[...], wide, preferred_element_type=F32)
            stacked = jnp.concatenate(
                [
                    jnp.concatenate(
                        [
                            (
                                rows[b * size : (b + 1) * size, j * size : (j + 1) * size]
                                * values[b]
                            ).astype(BF16)
                            for b in range(nb)
                        ],
                        axis=1,
                    )
                    for j, (_, _, values) in enumerate(pair)
                ],
                axis=0,
            )
            out = jnp.dot(stacked, col_cat[...], preferred_element_type=F32)
            for j, (_, key, values) in enumerate(pair):
                cell = key & (CELLS - 1)
                xp = key >> 7
                g = cell >> 3
                hh = (cell & (CELL_COLS - 1)) - h0
                for part in range(parts):
                    base = j * size + part * R
                    spot = acc.at[xp, g * parts + part, hh]
                    spot[...] = spot[...] + out[base : base + R]
                wrow = wacc.at[pl.ds(xp, 1), :]
                wrow[...] = wrow[...] + jnp.where(lane == cell, values[nb], 0.0)
        return carry

    lax.fori_loop(0, (n + UNROLL - 1) // UNROLL, step, jnp.int32(0))

    for j in range(X):
        xp = lax.rem(x + j, X)

        def put_a(v, carry, j=j, xp=xp):
            for hh in range(na):
                start = pl.multiple_of((v * na + hh) * R, 16)
                a_out[j][pl.ds(start, R), :] = acc[xp, v, hh].astype(BF16)
            return carry

        lax.fori_loop(0, V, put_a, jnp.int32(0))
        store_weights(a_out[j], V * na * R, wacc[pl.ds(xp, 1), :])
    for i in range(Y):
        yp = lax.rem(y + i, Y)
        for j in range(X):
            xp = lax.rem(x + j, X)

            def put_b(z, carry, i=i, j=j, xp=xp, yp=yp):
                for hh in range(nbc):
                    start = pl.multiple_of(((j * Z + z) * nbc + hh) * R, 16)
                    b_out[i][pl.ds(start, R), :] = acc[xp, z * Y + yp, na + hh].astype(BF16)
                return carry

            lax.fori_loop(0, Z, put_b, jnp.int32(0))


def first_add_kernel(scal, *refs, cfg, na, nbc):
    X, Y, Z, V, R, _, _ = cfg
    a_in = refs[:X]
    b_in = refs[X : X + Y]
    a_out = refs[X + Y : X + 2 * Y]
    b_out = refs[X + 2 * Y :]
    y = scal[3]
    w = sum(load_weights(ref, V * na * R) for ref in a_in)
    span = na * R
    for i in range(Y):
        yp = lax.rem(y + i, Y)
        for z in range(Z):
            start = pl.multiple_of((z * Y + yp) * span, 16)
            total = sum(ref[pl.ds(start, span), :].astype(F32) for ref in a_in)
            a_out[i][z * span : (z + 1) * span, :] = total.astype(BF16)
        store_weights(a_out[i], Z * span, w)
    block = Z * nbc * R
    for j in range(X):
        total = sum(ref[j * block : (j + 1) * block, :].astype(F32) for ref in b_in)
        b_out[j][...] = total.astype(BF16)


def second_add_kernel(scal, *refs, cfg, na, nbc):
    X, Y, Z, V, R, _, _ = cfg
    a_in = refs[:Y]
    b_in = refs[Y : Y + X]
    outs = refs[Y + X :]
    z = scal[2]
    w = sum(load_weights(ref, Z * na * R) for ref in a_in)
    for k in range(Z):
        zp = lax.rem(z + k, Z)
        start = pl.multiple_of(zp * (na * R), 16)
        total = sum(ref[pl.ds(start, na * R), :].astype(F32) for ref in a_in)
        outs[k][: na * R, :] = total.astype(BF16)
        start = pl.multiple_of(zp * (nbc * R), 16)
        total = sum(ref[pl.ds(start, nbc * R), :].astype(F32) for ref in b_in)
        outs[k][na * R : (na + nbc) * R, :] = total.astype(BF16)
        store_weights(outs[k], (na + nbc) * R, w)


def coadd_kernel(scal, *refs, cfg, h0, nh):
    X, Y, Z, V, R, _, _ = cfg
    ins = refs[:Z]
    out, top, bottom = refs[Z:]
    g = (scal[2] * Y + scal[3]) // (V // CELL_ROWS)
    w = sum(load_weights(ref, nh * R) for ref in ins)
    lane = lax.broadcasted_iota(jnp.int32, (1, 128), 1)
    for hh in range(nh):
        total = sum(ref[hh * R : (hh + 1) * R, :].astype(F32) for ref in ins)
        here = jnp.where(lane == g * CELL_COLS + h0 + hh, w, 0.0)
        denom = jnp.sum(here, axis=1, keepdims=True) + 1.0
        value = total / denom
        cols = slice(hh * 128, (hh + 1) * 128)
        out[:, cols] = value
        top[:, cols] = value[:EDGE].astype(BF16)
        bottom[:, cols] = value[R - EDGE :].astype(BF16)


def detect_kernel(vert, horiz, *refs, nsets, R):
    strips = refs[:nsets]
    aboves = refs[nsets : 2 * nsets]
    belows = refs[2 * nsets : 3 * nsets]
    coadd, detect = refs[3 * nsets : 3 * nsets + 2]
    filtered = refs[3 * nsets + 2]
    base = 0
    for strip, above, below in zip(strips, aboves, belows):
        width = strip.shape[1]
        coadd[:, base : base + width] = strip[...]
        extended = jnp.concatenate([above[...], strip[...].astype(BF16), below[...]], axis=0)
        filtered[:, base : base + width] = jnp.dot(
            vert[...], extended, preferred_element_type=F32
        ).astype(BF16)
        base += width
    blocks = base // 128
    for j in range(blocks):
        lo, hi = max(j - 1, 0), min(j + 2, blocks)
        detect[:, j * 128 : (j + 1) * 128] = jnp.dot(
            filtered[:, lo * 128 : hi * 128],
            horiz[(lo - j + 1) * 128 : (hi - j + 1) * 128, :],
            preferred_element_type=F32,
        )


def shards(
    warped_tiles,
    coefficients,
    tile_weight,
    tile_cell,
    tile_valid,
    dest_patch,
    basis_taps,
    filter_taps,
):
    count, size = warped_tiles.shape[:2]
    nb, _, nt = basis_taps.shape
    nf = filter_taps.shape[1]
    patches, V = lax.axis_size("patch"), lax.axis_size("visit")
    X, Y, Z = patches // 2, 2, V // 2
    R = CELL_ROWS * size // V
    cfg = (X, Y, Z, V, R, nb, count)
    patch, visit = lax.axis_index("patch"), lax.axis_index("visit")
    scal = jnp.stack([patch // 2, patch % 2, visit // 2, visit % 2]).astype(jnp.int32)

    def send(value, move):
        pairs = []
        for v in range(V):
            for p in range(patches):
                z, y, x, core = move(v // Y, v % Y, p // 2, p % 2)
                pairs.append((v * patches + p, (z * Y + y) * patches + x * 2 + core))
        return lax.ppermute(value, ("visit", "patch"), pairs)

    def to_core(value):
        return send(value, lambda z, y, x, core: (z, y, x, 1 - core))

    def to_x(value, k):
        return send(value, lambda z, y, x, core: (z, y, (x + k) % X, core))

    def to_y(value, k):
        return send(value, lambda z, y, x, core: (z, (y + k) % Y, x, core))

    def to_z(value, k):
        return send(value, lambda z, y, x, core: ((z + k) % Z, y, x, core))

    effective = lax.reduce_precision(
        tile_weight.astype(F32) * tile_valid.astype(F32), exponent_bits=8, mantissa_bits=7
    )
    scales = lax.reduce_precision(
        coefficients.astype(F32) * effective[:, None], exponent_bits=8, mantissa_bits=7
    )
    info = jnp.concatenate(
        [scales, effective[:, None], jnp.zeros((count, 7 - nb), F32)], axis=1
    ).reshape(count * 8)
    keys = dest_patch * CELLS + tile_cell
    tiles_other = to_core(warped_tiles)
    info_other = to_core(info)
    keys_other = to_core(keys)

    row_cat, col_cat = pl.pallas_call(
        functools.partial(basis_kernel, nb=nb, nt=nt, size=size),
        out_shape=(rows_shape(nb * size), rows_shape(nb * size)),
        in_specs=[in_smem()],
        out_specs=(in_vmem(), in_vmem()),
    )(basis_taps.astype(F32).reshape(-1))
    vert, horiz = pl.pallas_call(
        functools.partial(filter_mats_kernel, nt=nf, strip=R, pad=128),
        out_shape=(
            jax.ShapeDtypeStruct((R, R + 2 * EDGE), BF16),
            rows_shape(384),
        ),
        in_specs=[in_smem()],
        out_specs=(in_vmem(), in_vmem()),
    )(filter_taps.astype(F32).reshape(-1))

    strips, tops, bottoms = [], [], []
    for cols_a, cols_b in SETS:
        na, nbc = cols_a[1] - cols_a[0], cols_b[1] - cols_b[0]
        nh = na + nbc
        outs = pl.pallas_call(
            functools.partial(match_kernel, cfg=cfg, cols_a=cols_a, cols_b=cols_b),
            out_shape=tuple(
                [rows_shape(V * na * R + WROWS)] * X + [rows_shape(X * Z * nbc * R)] * Y
            ),
            in_specs=[in_smem()] * 5
            + [pl.BlockSpec(memory_space=pl.ANY)] * 2
            + [in_vmem()] * 2,
            out_specs=tuple([in_vmem()] * (X + Y)),
            scratch_shapes=[
                pltpu.VMEM((X, V, nh, R, 128), F32),
                pltpu.VMEM((max(X, 8), 128), F32),
                pltpu.SMEM((2 * count + UNROLL,), jnp.int32),
                pltpu.VMEM((2 * count, size, size), BF16),
                pltpu.SemaphoreType.DMA((2,)),
            ],
        )(
            scal,
            keys,
            keys_other,
            info,
            info_other,
            warped_tiles,
            tiles_other,
            row_cat,
            col_cat,
        )
        a, b = outs[:X], outs[X:]
        a = [a[0]] + [to_x(a[k], k) for k in range(1, X)]
        b = [b[0]] + [to_y(b[k], k) for k in range(1, Y)]
        outs = pl.pallas_call(
            functools.partial(first_add_kernel, cfg=cfg, na=na, nbc=nbc),
            out_shape=tuple(
                [rows_shape(Z * na * R + WROWS)] * Y + [rows_shape(Z * nbc * R)] * X
            ),
            in_specs=[in_smem()] + [in_vmem()] * (X + Y),
            out_specs=tuple([in_vmem()] * (X + Y)),
        )(scal, *a, *b)
        a, b = outs[:Y], outs[Y:]
        a = [a[0]] + [to_y(a[k], k) for k in range(1, Y)]
        b = [b[0]] + [to_x(b[k], k) for k in range(1, X)]
        outs = pl.pallas_call(
            functools.partial(second_add_kernel, cfg=cfg, na=na, nbc=nbc),
            out_shape=tuple([rows_shape(nh * R + WROWS)] * Z),
            in_specs=[in_smem()] + [in_vmem()] * (X + Y),
            out_specs=tuple([in_vmem()] * Z),
        )(scal, *a, *b)
        outs = [outs[0]] + [to_z(outs[k], k) for k in range(1, Z)]
        strip, top, bottom = pl.pallas_call(
            functools.partial(coadd_kernel, cfg=cfg, h0=cols_a[0], nh=nh),
            out_shape=(
                jax.ShapeDtypeStruct((R, nh * 128), F32),
                jax.ShapeDtypeStruct((EDGE, nh * 128), BF16),
                jax.ShapeDtypeStruct((EDGE, nh * 128), BF16),
            ),
            in_specs=[in_smem()] + [in_vmem()] * Z,
            out_specs=(in_vmem(), in_vmem(), in_vmem()),
        )(scal, *outs)
        strips.append(strip)
        tops.append(top)
        bottoms.append(bottom)
    aboves = [lax.ppermute(v, "visit", [(i, i + 1) for i in range(V - 1)]) for v in bottoms]
    belows = [lax.ppermute(v, "visit", [(i + 1, i) for i in range(V - 1)]) for v in tops]
    nsets = len(SETS)
    coadd, detect = pl.pallas_call(
        functools.partial(detect_kernel, nsets=nsets, R=R),
        out_shape=(
            jax.ShapeDtypeStruct((R, CELL_COLS * size), F32),
            jax.ShapeDtypeStruct((R, CELL_COLS * size), F32),
        ),
        in_specs=[in_vmem()] * (2 + 3 * nsets),
        out_specs=(in_vmem(), in_vmem()),
        scratch_shapes=[pltpu.VMEM((R, CELL_COLS * size), BF16)],
    )(vert, horiz, *strips, *aboves, *belows)
    return coadd[None], detect[None]


def solution(mesh):
    in_specs = (
        P(("visit", "patch"), None, None),
        P(("visit", "patch"), None),
        P(("visit", "patch")),
        P(("visit", "patch")),
        P(("visit", "patch")),
        P(("visit", "patch")),
        P(),
        P(),
    )
    out_specs = (P("patch", "visit", None), P("patch", "visit", None))
    return jax.shard_map(shards, mesh=mesh, in_specs=in_specs, out_specs=out_specs, check_vma=False)
```

```python
import functools

import jax
import jax.numpy as jnp
from jax import lax
from jax.experimental import pallas as pl
from jax.experimental.pallas import tpu as pltpu
from jax.sharding import PartitionSpec as P

CELL_ROWS = 8
CELL_COLS = 8
CELLS = CELL_ROWS * CELL_COLS
SETS = ((0, 4), (4, 8))
UNROLL = 8
EDGE = 32
WKEEP = 8
WSEND = 32
F32 = jnp.float32
BF16 = jnp.bfloat16
VMEM = pl.BlockSpec(memory_space=pltpu.VMEM)
SMEM = pl.BlockSpec(memory_space=pltpu.SMEM)
ANY = pl.BlockSpec(memory_space=pl.ANY)


def rows_shape(rows, dtype=BF16):
    return jax.ShapeDtypeStruct((rows, 128), dtype)


def turned(row, ncols, shift):
    full = pltpu.roll(jnp.broadcast_to(row, (128, ncols)), shift % ncols, 1)
    return pltpu.roll(full, 0, 1, stride=1, stride_axis=0)


def mats_kernel(basis, filt, row_out, col_out, vert_out, horiz_out, *, nb, nt, nf, size, strip):
    reach = (nt - 1) // 2
    row = lax.broadcasted_iota(jnp.int32, (size, size), 0)
    col = lax.broadcasted_iota(jnp.int32, (size, size), 1)
    near = jnp.abs(col - row) <= reach
    for b in range(nb):
        block = slice(b * size, (b + 1) * size)
        taps = basis[b : b + 1, :]
        row_out[:, block] = jnp.where(near, turned(taps, size, -reach), 0.0).astype(BF16)
        taps = basis[nb + b : nb + b + 1, :]
        col_out[:, block] = jnp.where(near, turned(taps, size, -reach), 0.0).astype(BF16)
    reach = (nf - 1) // 2
    taps = jnp.concatenate([filt[0:1, :], jnp.zeros((1, 128), F32)], axis=1)
    vert_out[...] = turned(taps, 256, EDGE - reach)[:strip, : strip + 2 * EDGE].astype(BF16)
    for k in range(3):
        inside = jnp.abs((k - 1) * size + row - col) <= reach
        taps = jnp.where(inside, turned(filt[1:2, :], size, -reach), 0.0)
        horiz_out[k * size : (k + 1) * size, :] = taps.astype(BF16)


def pack_weights(w):
    hi = w.astype(BF16)
    rest = w - hi.astype(F32)
    mid = rest.astype(BF16)
    lo = (rest - mid.astype(F32)).astype(BF16)
    parts = [hi.astype(F32), mid.astype(F32), lo.astype(F32), jnp.zeros_like(w)]
    return jnp.concatenate(parts, axis=0).astype(BF16)


def unpack_weights(block):
    block = block.astype(F32)
    return block[0:8] + block[8:16] + block[16:24]


def pick(swap, a, b):
    return jnp.where(swap, b, a), jnp.where(swap, a, b)


def match_kernel(scal, info_own, info_other, tiles_own, tiles_other, row_cat, col_cat, *refs, cfg, h0, nh):
    X, Y, Z, R, nb, count, n1, n2 = cfg
    acc, wacc = refs[:2]
    sends = refs[2 : 1 + n1]
    listing, scaled, own_s, other_s, sems = refs[1 + n1 :]
    size = tiles_own.shape[1]
    parts = size // R
    x, core, y, swap = scal[0], scal[1], scal[3], scal[4] > 0
    loads = [
        pltpu.make_async_copy(info_own, own_s, sems.at[0]),
        pltpu.make_async_copy(info_other, other_s, sems.at[1]),
    ]
    for copy in loads:
        copy.start()
    acc[...] = jnp.zeros_like(acc)
    wacc[...] = jnp.zeros_like(wacc)
    scaled[1] = jnp.zeros_like(scaled[1])
    for copy in loads:
        copy.wait()

    def lister(info, base):
        def body(t, n):
            key = info[6, t].astype(jnp.int32)
            h = key & (CELL_COLS - 1)
            mine = (((key >> 6) & 1) == core) & (h >= h0) & (h < h0 + nh)
            listing[n] = base + t
            return n + mine.astype(jnp.int32)

        return body

    n = lax.fori_loop(0, count, lister(own_s, 0), jnp.int32(0), unroll=8)
    n = lax.fori_loop(0, count, lister(other_s, count), n, unroll=8)
    for q in range(UNROLL):
        listing[n + q] = 0
    lane = lax.broadcasted_iota(jnp.int32, (1, 128), 1)

    def fetch(k, what):
        t = listing[jnp.clip(k, 0, n)]
        own = t < count
        t_in = jnp.where(own, t, t - count)
        return own, t_in, [jnp.where(own, own_s[b, t_in], other_s[b, t_in]) for b in what]

    def step(i, carry):
        now = i & 1
        for q in range(0, UNROLL, 2):
            pair, tall = [], []
            for k in (i * UNROLL + q, i * UNROLL + q + 1):
                own, t, values = fetch(k, range(nb))
                pair.append([jnp.where(k < n, v, 0.0) for v in values])
                tall.append(jnp.where(own, tiles_own[t], tiles_other[t]))
            tall = jnp.concatenate(tall, axis=0)
            cols = jnp.dot(tall, col_cat[...], preferred_element_type=F32)
            for j, values in enumerate(pair):
                for b in range(nb):
                    part = cols[j * size : (j + 1) * size, b * size : (b + 1) * size] * values[b]
                    scaled[now, b * size : (b + 1) * size, (q + j) * size : (q + j + 1) * size] = (
                        part.astype(BF16)
                    )
        for q in range(0, UNROLL, 2):
            wide = scaled[1 - now, :, q * size : (q + 2) * size]
            out = jnp.dot(row_cat[...], wide, preferred_element_type=F32)
            for j in range(2):
                k = (i - 1) * UNROLL + q + j
                live = (k >= 0) & (k < n)
                _, _, (weight, key) = fetch(k, (nb, 6))
                key = jnp.where(live, key.astype(jnp.int32), h0)
                cell = key & (CELLS - 1)
                xp = key >> 7
                g = cell >> 3
                hh = (cell & (CELL_COLS - 1)) - h0
                for part in range(parts):
                    v = g * parts + part
                    spot = acc.at[xp, lax.rem(v, Y), v // Y, hh]
                    spot[...] = spot[...] + out[part * R : (part + 1) * R, j * size : (j + 1) * size]
                wrow = wacc.at[pl.ds(xp, 1), :]
                wrow[...] = wrow[...] + jnp.where((lane == cell) & live, weight, 0.0)
        return carry

    lax.fori_loop(0, (n + UNROLL - 1) // UNROLL + 1, step, jnp.int32(0))

    me = jnp.where(swap, y, x)
    block = Z * nh * R
    for i in range(1, n1):
        a = lax.rem(me + i, n1)
        for b in range(n2):
            xp, yp = pick(swap, a, b)
            for z in range(Z):
                for hh in range(nh):
                    start = b * block + (z * nh + hh) * R
                    sends[i - 1][start : start + R, :] = acc[xp, yp, z, hh].astype(BF16)
        sends[i - 1][n2 * block : n2 * block + WSEND, :] = pack_weights(wacc[...])


def first_add_kernel(scal, acc, wacc, *refs, cfg, nh):
    X, Y, Z, R, _, _, n1, n2 = cfg
    others = refs[: n1 - 1]
    keep, wkeep = refs[n1 - 1 : n1 + 1]
    sends = refs[n1 + 1 :]
    swap = scal[4] > 0
    first, second = jnp.where(swap, scal[3], scal[0]), jnp.where(swap, scal[0], scal[3])
    block = Z * nh * R
    w = wacc[...]
    for other in others:
        w = w + unpack_weights(other[n2 * block : n2 * block + WSEND])
    wkeep[...] = w
    for j in list(range(1, n2)) + [0]:
        b = lax.rem(second + j, n2)
        xp, yp = pick(swap, first, b)
        for z in range(Z):
            for hh in range(nh):
                at = (z * nh + hh) * R
                start = pl.multiple_of(b * block + at, 32)
                total = acc[xp, yp, z, hh]
                for other in others:
                    total = total + other[pl.ds(start, R), :].astype(F32)
                if j:
                    sends[j - 1][at : at + R, :] = total.astype(BF16)
                else:
                    keep[z, hh] = total
        if j:
            sends[j - 1][block : block + WSEND, :] = pack_weights(w)


def second_add_kernel(scal, kept, wkept, *refs, cfg, nh):
    X, Y, Z, R, _, _, n1, n2 = cfg
    others = refs[: n2 - 1]
    keep, wkeep = refs[n2 - 1 : n2 + 1]
    sends = refs[n2 + 1 :]
    w = wkept[...]
    for other in others:
        w = w + unpack_weights(other[Z * nh * R : Z * nh * R + WSEND])
    wkeep[...] = w
    for k in list(range(1, Z)) + [0]:
        z = lax.rem(scal[2] + k, Z)
        for hh in range(nh):
            start = pl.multiple_of((z * nh + hh) * R, 32)
            total = kept[z, hh]
            for other in others:
                total = total + other[pl.ds(start, R), :].astype(F32)
            if k:
                sends[k - 1][hh * R : (hh + 1) * R, :] = total.astype(BF16)
            else:
                keep[hh] = total
        if k:
            sends[k - 1][nh * R : nh * R + WSEND, :] = pack_weights(w)


def coadd_kernel(scal, kept, wkept, *refs, cfg, h0, nh, last):
    X, Y, Z, R = cfg[:4]
    others = refs[: Z - 1]
    befores = refs[Z - 1 : -3] if last else ()
    strip = refs[-3] if last else refs[-1]
    w = wkept[...]
    for other in others:
        w = w + unpack_weights(other[nh * R : nh * R + WSEND])
    g = (scal[2] * Y + scal[3]) // (Y * Z // CELL_ROWS)
    lane = lax.broadcasted_iota(jnp.int32, (WKEEP, 128), 1)
    patch = lax.broadcasted_iota(jnp.int32, (WKEEP, 128), 0)
    for hh in range(nh):
        total = kept[hh]
        for other in others:
            total = total + other[hh * R : (hh + 1) * R].astype(F32)
        here = (patch == scal[0]) & (lane == g * CELL_COLS + h0 + hh)
        denom = jnp.sum(jnp.where(here, w, 0.0)) + 1.0
        strip[:, hh * 128 : (hh + 1) * 128] = total / denom
    if last:
        top, bottom = refs[-2:]
        base = 0
        for part in list(befores) + [strip]:
            cols = slice(base, base + part.shape[1])
            top[:, cols] = part[:EDGE].astype(BF16)
            bottom[:, cols] = part[R - EDGE :].astype(BF16)
            base += part.shape[1]


def detect_kernel(vert, horiz, above, below, *refs):
    parts = refs[:-3]
    coadd, detect, filtered = refs[-3:]
    base = 0
    for part in parts:
        cols = slice(base, base + part.shape[1])
        coadd[:, cols] = part[...]
        extended = jnp.concatenate(
            [above[:, cols], part[...].astype(BF16), below[:, cols]], axis=0
        )
        filtered[:, cols] = jnp.dot(vert[...], extended, preferred_element_type=F32).astype(BF16)
        base += part.shape[1]
    blocks = base // 128
    for j in range(blocks):
        lo, hi = max(j - 1, 0), min(j + 2, blocks)
        detect[:, j * 128 : (j + 1) * 128] = jnp.dot(
            filtered[:, lo * 128 : hi * 128],
            horiz[(lo - j + 1) * 128 : (hi - j + 1) * 128, :],
            preferred_element_type=F32,
        )


def shards(
    warped_tiles,
    coefficients,
    tile_weight,
    tile_cell,
    tile_valid,
    dest_patch,
    basis_taps,
    filter_taps,
):
    count, size = warped_tiles.shape[:2]
    nb, _, nt = basis_taps.shape
    nf = filter_taps.shape[1]
    patches, V = lax.axis_size("patch"), lax.axis_size("visit")
    X, Y, Z = patches // 2, 2, V // 2
    R = CELL_ROWS * size // V
    crossed = X == Y
    n1, n2 = X, Y
    cfg = (X, Y, Z, R, nb, count, n1, n2)
    patch, visit = lax.axis_index("patch"), lax.axis_index("visit")
    x, core, z, y = patch // 2, patch % 2, visit // Y, visit % Y
    swap = core if crossed else core * 0
    scal = jnp.stack([x, core, z, y, swap]).astype(jnp.int32)

    def send(value, move):
        pairs = []
        for v in range(V):
            for p in range(patches):
                z, y, x, core = move(v // Y, v % Y, p // 2, p % 2)
                pairs.append((v * patches + p, (z * Y + y) * patches + x * 2 + core))
        return lax.ppermute(value, ("visit", "patch"), pairs)

    def to_core(value):
        return send(value, lambda z, y, x, core: (z, y, x, 1 - core))

    def hop(value, k, first):
        def move(z, y, x, core):
            if first != (crossed and core == 1):
                return z, y, (x + k) % X, core
            return z, (y + k) % Y, x, core

        return send(value, move)

    def to_z(value, k):
        return send(value, lambda z, y, x, core: ((z + k) % Z, y, x, core))

    tiles_other = to_core(warped_tiles)
    effective = lax.reduce_precision(
        tile_weight.astype(F32) * tile_valid.astype(F32), exponent_bits=8, mantissa_bits=7
    )
    scales = lax.reduce_precision(
        coefficients.T.astype(F32) * effective[None, :], exponent_bits=8, mantissa_bits=7
    )
    keys = (dest_patch * CELLS + tile_cell).astype(F32)
    info = jnp.concatenate(
        [scales, effective[None], jnp.zeros((5 - nb, count), F32), keys[None], keys[None]], axis=0
    )
    info = jnp.pad(info, ((0, 0), (0, 128 - count)))
    info_other = to_core(info)

    basis = jnp.concatenate([basis_taps[:, 0, :], basis_taps[:, 1, ::-1]], axis=0).astype(F32)
    filt = jnp.concatenate([filter_taps[:1], filter_taps[1:, ::-1]], axis=0).astype(F32)
    basis = jnp.pad(basis, ((0, 0), (0, 128 - nt)))
    filt = jnp.pad(filt, ((0, 0), (0, 128 - nf)))
    fast = crossed
    limit = pltpu.CompilerParams(vmem_limit_bytes=12 << 20) if fast else None

    def array(shape, dtype):
        return pltpu.VMEM(shape, dtype) if fast else jax.ShapeDtypeStruct(shape, dtype)

    def near(value):
        return pltpu.with_memory_space_constraint(value, pltpu.VMEM) if fast else value

    def call(kernel, name, small, arrays, outs, scratch=()):
        return pl.pallas_call(
            kernel,
            out_shape=tuple(array(*out) for out in outs),
            in_specs=[SMEM] * len(small) + [VMEM] * len(arrays),
            out_specs=tuple([VMEM] * len(outs)),
            scratch_shapes=list(scratch),
            compiler_params=limit,
            name=name,
        )(*small, *[near(value) for value in arrays])

    row_cat, col_cat, vert, horiz = call(
        functools.partial(mats_kernel, nb=nb, nt=nt, nf=nf, size=size, strip=R),
        "mats",
        [],
        [basis, filt],
        [
            ((size, nb * size), BF16),
            ((size, nb * size), BF16),
            ((R, R + 2 * EDGE), BF16),
            ((3 * size, 128), BF16),
        ],
    )
    strips = []
    for index, (h0, h1) in enumerate(SETS):
        nh = h1 - h0
        block = Z * nh * R
        weights = ((WKEEP, 128), F32)
        acc, w, *sends = call(
            functools.partial(match_kernel, cfg=cfg, h0=h0, nh=nh),
            f"match{index}",
            [scal],
            [info, info_other, warped_tiles, tiles_other, row_cat, col_cat],
            [((X, Y, Z, nh, R, 128), F32), weights]
            + [((n2 * block + WSEND, 128), BF16)] * (n1 - 1),
            [
                pltpu.SMEM((2 * count + UNROLL,), jnp.int32),
                pltpu.VMEM((2, nb * size, UNROLL * size), BF16),
                pltpu.SMEM((8, 128), F32),
                pltpu.SMEM((8, 128), F32),
                pltpu.SemaphoreType.DMA((2,)),
            ],
        )
        others = [hop(value, k + 1, True) for k, value in enumerate(sends)]
        keep, w, *sends = call(
            functools.partial(first_add_kernel, cfg=cfg, nh=nh),
            f"add1_{index}",
            [scal],
            [acc, w, *others],
            [((Z, nh, R, 128), F32), weights] + [((block + WSEND, 128), BF16)] * (n2 - 1),
        )
        others = [hop(value, k + 1, False) for k, value in enumerate(sends)]
        keep, w, *sends = call(
            functools.partial(second_add_kernel, cfg=cfg, nh=nh),
            f"add2_{index}",
            [scal],
            [keep, w, *others],
            [((nh, R, 128), F32), weights] + [((nh * R + WSEND, 128), BF16)] * (Z - 1),
        )
        others = [to_z(value, k + 1) for k, value in enumerate(sends)]
        last = index == len(SETS) - 1
        strip, *edges = call(
            functools.partial(coadd_kernel, cfg=cfg, h0=h0, nh=nh, last=last),
            f"coadd{index}",
            [scal],
            [keep, w, *others] + (strips if last else []),
            [((R, nh * 128), F32)] + ([((EDGE, CELL_COLS * size), BF16)] * 2 if last else []),
        )
        strips.append(strip)
    top, bottom = edges
    above = lax.ppermute(bottom, "visit", [(i, i + 1) for i in range(V - 1)])
    below = lax.ppermute(top, "visit", [(i + 1, i) for i in range(V - 1)])
    arrays = [vert, horiz, above, below, *strips]
    coadd, detect = pl.pallas_call(
        detect_kernel,
        out_shape=(
            jax.ShapeDtypeStruct((R, CELL_COLS * size), F32),
            jax.ShapeDtypeStruct((R, CELL_COLS * size), F32),
        ),
        in_specs=[VMEM] * len(arrays),
        out_specs=(VMEM, VMEM),
        scratch_shapes=[pltpu.VMEM((R, CELL_COLS * size), BF16)],
        compiler_params=limit,
        name="detect",
    )(*[near(value) for value in arrays])
    return coadd[None], detect[None]


def solution(mesh):
    in_specs = (
        P(("visit", "patch"), None, None),
        P(("visit", "patch"), None),
        P(("visit", "patch")),
        P(("visit", "patch")),
        P(("visit", "patch")),
        P(("visit", "patch")),
        P(),
        P(),
    )
    out_specs = (P("patch", "visit", None), P("patch", "visit", None))
    return jax.shard_map(shards, mesh=mesh, in_specs=in_specs, out_specs=out_specs, check_vma=False)
```
